128 devices in a mesh: lag: 16 (over z_lo, x, core), row: 8 (over y, z_hi).
Axes of the slice: x: 4, y: 4, z: 4 (z_hi: 2, z_lo: 2; z = z_hi * 2 + z_lo), core: 2. Of those that a mesh axis runs over, the one named last changes fastest.
Arguments:
- lag_matrix: bfloat16 [16, 8192, 8192], P('lag', 'row'), may hold values from -0.015625 to 0.015625
- past_current: bfloat16 [16, 256, 8192], P('lag', None, 'row'), may hold values from -6 to 6
- excitation: float32 [2, 256, 8192], P(None, None, 'row'), may hold values from -6 to 6
- block_inverse: float32 [64, 128, 128], P('row'), may hold values from -2 to 3
Outputs:
- currents: bfloat16 [2, 256, 8192], P(None, 'lag', 'row')
The draws below stay inside these ranges and needn't reach their ends.
All inputs are finite; a program needn't handle non-finite values.
Results may differ from the reference program's by a relative error of at most 0.002.
Values may be sent and summed in bfloat16 or wider, within the bound.
A program may use at most 64 MiB of HBM per device.

```python
import jax
import jax.numpy as jnp
from jax import lax

N = 8192
BLOCK = 128
EXCITE = 256
STEPS = 2
LAGS = 16


def draw_block_inverse(key, part):
    inner = jax.random.fold_in(key, 11)
    shape = (N // BLOCK, BLOCK, BLOCK)
    spread = jax.random.normal(inner, shape, jnp.float32) * (0.5 / BLOCK ** 0.5)
    spread = jnp.clip(spread, -0.9, 0.9)
    return spread + jnp.eye(BLOCK, dtype=jnp.float32)[None]


def levels(own_key, extent, cuts, low, high):
    factor_of, own = 1.0, jax.random.fold_in(own_key, 6)
    for position, parts in cuts:
        draws = jnp.exp(jax.random.uniform(jax.random.fold_in(own, position), (parts,), jnp.float32, low / len(cuts), high / len(cuts)))
        factor_of = factor_of * jnp.repeat(draws, extent[position] // parts).reshape([-1 if axis == position else 1 for axis in range(len(extent))])
    return factor_of


def normal_values(own_key, dims, scale, limit, shards=(), held_as=jnp.bfloat16):
    values = scale * jax.random.normal(own_key, dims, jnp.float32)
    if shards:
        values = values * levels(own_key, dims, shards, -0.22, 0.18)
    return jnp.clip(values, -limit, limit).astype(held_as)


def setup_inputs(seed: int = 0) -> dict:
    arg_keys = jax.random.split(jax.random.key(seed), 5)
    lag_matrix = normal_values(arg_keys[0], (LAGS, N, N), (N * LAGS) ** -0.5, 0.015625, ((0, 16), (1, 8)))
    past_current = normal_values(arg_keys[1], (LAGS, EXCITE, N), 1.0, 6.0, ((0, 16), (2, 8)))
    excitation = normal_values(arg_keys[2], (STEPS, EXCITE, N), 1.0, 6.0, ((2, 8),), jnp.float32)
    block_inverse = draw_block_inverse(jax.random.fold_in(arg_keys[4], 71), 0)
    return dict(lag_matrix=lag_matrix, past_current=past_current, excitation=excitation, block_inverse=block_inverse)


def solve_blocks(source, block_inverse):
    pieces = source.reshape(EXCITE, N // BLOCK, BLOCK)
    result = jnp.einsum("bij,rbj->rbi", block_inverse, pieces, precision=lax.Precision.HIGHEST)
    return result.reshape(EXCITE, N).astype(jnp.bfloat16)


def reference(lag_matrix, past_current, excitation, block_inverse):
    history_cur = past_current
    results = []
    for step in range(STEPS):
        def add_lag(total, pair):
            matrix, current = pair
            return total + jnp.dot(current, matrix.T, preferred_element_type=jnp.float32), None

        history, _ = lax.scan(add_lag, jnp.zeros((EXCITE, N), jnp.float32), (lag_matrix, history_cur))
        source = excitation[step] - history
        newest = solve_blocks(source, block_inverse)
        results.append(newest)
        history_cur = jnp.concatenate([newest[None], history_cur[:-1]], axis=0)
    return jnp.stack(results)
```

```python
import jax
import jax.numpy as jnp
from jax import lax
from jax.experimental import pallas as pl
from jax.experimental.pallas import tpu as pltpu
from jax.sharding import PartitionSpec as P

MESH = pl.DeviceIdType.MESH
NT = (((1,), (1,)), ((), ()))
F32 = jnp.float32


def kernel(m_hbm, p_hbm, e_hbm, b_hbm, out_ref, mv, g, tg, acc, acc2, xbuf, part, rbuf, ex, binv, newest,
           m_sem, loc_sem, ga_s, ga_r, gt_s, gt_r, sib_s, sib_r, sh_s, sh_r, x_s, x_r, rs_s, rs_r, nb_s, nb_r):
    lag, row = lax.axis_index("lag"), lax.axis_index("row")
    core, x, zl = lag % 2, (lag // 2) % 4, lag // 8
    y, h = row // 2, row % 2
    yp, ym, y2, ho = (y + 1) % 4, (y + 3) % 4, (y + 2) % 4, 1 - h
    E, W = p_hbm.shape[1], p_hbm.shape[2]
    S = ex.shape[1]
    rows = {"0": (0, E // 2), "0a": (0, E // 4), "0b": (E // 4, E // 4),
            "1": (E // 2, E // 2), "1a": (E // 2, E // 4), "1b": (3 * E // 4, E // 4)}

    def lag_of(x_, zl_, c_):
        return (zl_ * 4 + x_) * 2 + c_

    def slot(y_, h_):
        return y_ * 2 + h_

    barrier = pltpu.get_barrier_semaphore()
    for peer in (slot(yp, h), slot(ym, h), slot(y, ho)):
        pl.semaphore_signal(barrier, 1, device_id={"row": peer}, device_id_type=MESH)
    for k in range(1, 16):
        pl.semaphore_signal(barrier, 1, device_id={"lag": (lag + k) % 16}, device_id_type=MESH)

    order = [(y, h), (ym, h), (yp, h), (y, ho), (y2, h), (ym, ho), (yp, ho), (y2, ho)]
    loads = [pltpu.make_async_copy(p_hbm.at[0], g.at[row], loc_sem.at[0]),
             pltpu.make_async_copy(e_hbm.at[:, pl.ds(pl.multiple_of(lag * S, S), S)], ex, loc_sem.at[1]),
             pltpu.make_async_copy(b_hbm, binv, loc_sem.at[2])]
    loads[0].start()
    m_loads = []
    for k, (y_, h_) in enumerate(order):
        s = slot(y_, h_)
        m_loads.append(pltpu.make_async_copy(m_hbm.at[0, :, pl.ds(pl.multiple_of(s * W, W), W)], mv.at[s], m_sem.at[k]))
        m_loads[-1].start()
    loads[1].start()
    loads[2].start()
    pl.semaphore_wait(barrier, 18)

    def mm(dst, src, s, first):
        @pl.loop(0, 4)
        def _(n):
            cols = pl.ds(pl.multiple_of(n * (W // 4), W // 4), W // 4)
            v = lax.dot_general(src[s], mv[s, cols, :], NT, preferred_element_type=F32)
            if first:
                dst[:, cols] = v
            else:
                dst[:, cols] += v

    def gather(buf, own, ss, rs, on_shard):
        zp, to_p, to_m = slot(y, ho), slot(yp, h), slot(ym, h)
        sends = [((y, h), "0", to_p), ((y, h), "0", to_m), ((ym, h), "0a", to_p), ((yp, h), "0b", to_m),
                 ((y, h), "0", zp), ((ym, h), "0", zp), ((yp, h), "0", zp), ((y2, h), "0a", zp), ((y2, h), "0b", zp),
                 ((y, h), "1", to_p), ((y, h), "1", to_m), ((ym, h), "1a", to_p), ((yp, h), "1b", to_m),
                 ((y, h), "1", zp), ((y, ho), "1", to_p), ((y, ho), "1", to_m), ((ym, ho), "1a", to_p), ((yp, ho), "1b", to_m)]
        arrivals = [((ym, h), "0"), ((yp, h), "0"), ((y2, h), "0a"), ((y2, h), "0b"),
                    ((y, ho), "0"), ((ym, ho), "0"), ((yp, ho), "0"), ((y2, ho), "0a"), ((y2, ho), "0b"),
                    ((ym, h), "1"), ((yp, h), "1"), ((y2, h), "1a"), ((y2, h), "1b"),
                    ((y, ho), "1"), ((ym, ho), "1"), ((yp, ho), "1"), ((y2, ho), "1a"), ((y2, ho), "1b")]
        started = []

        def start(*which):
            for i in which:
                (y_, h_), rr, to = sends[i]
                lo, n = rows[rr]
                s = slot(y_, h_)
                src = own.at[pl.ds(lo, n)] if i in (0, 1, 4, 9, 10, 13) else buf.at[s, pl.ds(lo, n)]
                cp = pltpu.make_async_remote_copy(src, buf.at[s, pl.ds(lo, n)], ss.at[i], rs.at[i],
                                                  device_id={"row": to}, device_id_type=MESH)
                cp.start()
                started.append(cp)

        def wait(*which):
            for i in which:
                (y_, h_), rr = arrivals[i]
                lo, n = rows[rr]
                s = slot(y_, h_)
                ref = buf.at[s, pl.ds(lo, n)]
                pltpu.make_async_remote_copy(ref, ref, ss.at[i], rs.at[i], device_id={"row": sends[i][2]},
                                             device_id_type=MESH).wait_recv()

        start(13, 0, 1, 9, 10, 4)
        on_shard(0)
        yield
        wait(13)
        start(14, 15)
        wait(0)
        start(2, 5)
        wait(1)
        start(3, 6)
        wait(9)
        start(11)
        on_shard(1)
        wait(10)
        start(12)
        on_shard(2)
        yield
        wait(4)
        on_shard(3)
        wait(2)
        start(7)
        wait(3)
        start(8)
        wait(14)
        start(16)
        wait(15)
        start(17)
        yield
        wait(11, 12)
        on_shard(4)
        wait(5)
        on_shard(5)
        wait(6)
        on_shard(6)
        wait(7, 8, 16, 17)
        on_shard(7)
        for cp in started:
            cp.wait_send()

    def sibling_copy(s, k):
        return pltpu.make_async_remote_copy(g.at[s], tg.at[s], sib_s.at[k], sib_r.at[k],
                                            device_id={"lag": lag + 1 - 2 * core}, device_id_type=MESH)

    shift = pltpu.make_async_remote_copy(p_hbm.at[0], tg.at[row], sh_s.at[0], sh_r.at[0],
                                         device_id={"lag": (lag + 1) % 16}, device_id_type=MESH)

    def a_shard(k):
        s = slot(*order[k])
        if k == 0:
            loads[0].wait()

        @pl.when(core == 0)
        def _():
            sibling_copy(s, k).start()
        m_loads[k].wait()
        mm(acc, g, s, k == 0)

    stages = gather(g, p_hbm.at[0], ga_s, ga_r, a_shard)
    next(stages)

    @pl.when((core == 1) & (lag < 15))
    def _():
        shift.start()
    for _ in stages:
        pass

    def reduce_and_solve(step, total, between):
        chips = [(dx, dz) for dx in (1, 3, 2, 0) for dz in (0, 1)]
        chips = [c for c in chips if c != (0, 0)] + [(0, 0)]

        def rows_of(k, c_):
            dx, dz = chips[k]
            return pl.ds(pl.multiple_of(lag_of((x + dx) % 4, (zl + dz) % 2, c_) * S, S), S)

        pair = []
        for k in range(8):
            cp = pltpu.make_async_remote_copy(total.at[rows_of(k, 1 - core)], xbuf.at[step, k], x_s.at[step, k], x_r.at[step, k],
                                              device_id={"lag": lag + 1 - 2 * core}, device_id_type=MESH)
            cp.start()
            pair.append(cp)
        sent = []
        for k in range(8):
            pair[k].wait_recv()
            part[step, k] = total[rows_of(k, core), :] + xbuf[step, k]
            if k < 7:
                dx, dz = chips[k]
                cp = pltpu.make_async_remote_copy(part.at[step, k], rbuf.at[step, k], rs_s.at[step, k], rs_r.at[step, k],
                                                  device_id={"lag": lag_of((x + dx) % 4, (zl + dz) % 2, core)}, device_id_type=MESH)
                cp.start()
                sent.append(cp)
        between()
        history = part[step, 7]
        for k in range(7):
            sent[k].wait_recv()
            history = history + rbuf[step, k]
        source = ex[step] - history
        for b in range(binv.shape[0]):
            cols = pl.ds(b * 128, 128)
            v = lax.dot_general(source[:, b * 128:(b + 1) * 128], binv[b], NT, precision=lax.Precision.HIGHEST,
                                preferred_element_type=F32)
            newest[:, cols] = v.astype(newest.dtype)
        out_ref[step] = newest[...]
        return pair + sent

    older = (core == 0) & (lag > 0)

    def t_shard(k):
        if k in (2, 3, 4, 7):
            return

    t_stages = gather(tg, tg.at[row], gt_s, gt_r, lambda k: None)

    loads[1].wait()
    loads[2].wait()
    sends = reduce_and_solve(0, acc, lambda: None)

    mine = pl.ds(pl.multiple_of(lag * S, S), S)
    to_first = pltpu.make_async_remote_copy(newest, tg.at[row, mine], nb_s.at[0], nb_r.at[lag],
                                            device_id={"lag": 0}, device_id_type=MESH)

    @pl.when(lag > 0)
    def _():
        to_first.start()

    @pl.when(older)
    def _():
        shift.wait_recv()
        for _ in gather(tg, tg.at[row], gt_s, gt_r, lambda k: None):
            pass

        @pl.loop(0, 8)
        def _(s):
            @pl.when(s == 0)
            def _():
                mm(acc2, tg, s, True)

            @pl.when(s > 0)
            def _():
                mm(acc2, tg, s, False)

    @pl.when(core == 1)
    def _():
        for k in range(8):
            s = slot(*order[k])
            sibling_copy(s, k).wait_recv()
            mm(acc2, tg, s, k == 0)

    @pl.when(lag == 0)
    def _():
        tg[row, mine, :] = newest[...]
        for l in range(1, 16):
            ref = tg.at[row, pl.ds(l * S, S)]
            pltpu.make_async_remote_copy(ref, ref, nb_s.at[0], nb_r.at[l], device_id={"lag": l}, device_id_type=MESH).wait_recv()
        for _ in gather(tg, tg.at[row], gt_s, gt_r, lambda k: mm(acc2, tg, slot(*order[k]), k == 0)):
            pass

    @pl.when(lag > 0)
    def _():
        to_first.wait_send()
    sends += reduce_and_solve(1, acc2, lambda: None)

    for cp in sends:
        cp.wait_send()

    @pl.when(core == 0)
    def _():
        for k in range(8):
            sibling_copy(slot(*order[k]), k).wait_send()

    @pl.when((core == 1) & (lag < 15))
    def _():
        shift.wait_send()


def per_device(lag_matrix, past_current, excitation, block_inverse):
    E, W = past_current.shape[1:]
    S = E // 16
    nb = block_inverse.shape[0]
    bf = past_current.dtype
    dma = pltpu.SemaphoreType.DMA
    return pl.pallas_call(
        kernel,
        out_shape=jax.ShapeDtypeStruct((2, S, W), bf),
        in_specs=[pl.BlockSpec(memory_space=pl.ANY)] * 4,
        out_specs=pl.BlockSpec(memory_space=pltpu.VMEM),
        scratch_shapes=[
            pltpu.VMEM((8, W, W), bf), pltpu.VMEM((8, E, W), bf), pltpu.VMEM((8, E, W), bf),
            pltpu.VMEM((E, W), F32), pltpu.VMEM((E, W), F32),
            pltpu.VMEM((2, 8, S, W), F32), pltpu.VMEM((2, 8, S, W), F32), pltpu.VMEM((2, 7, S, W), F32),
            pltpu.VMEM((2, S, W), F32), pltpu.VMEM((nb, 128, 128), F32), pltpu.VMEM((S, W), bf),
            dma((8,)), dma((3,)), dma((18,)), dma((18,)), dma((18,)), dma((18,)), dma((8,)), dma((8,)), dma((1,)), dma((1,)),
            dma((2, 8)), dma((2, 8)), dma((2, 7)), dma((2, 7)), dma((1,)), dma((16,)),
        ],
        compiler_params=pltpu.CompilerParams(collective_id=0, has_side_effects=True, vmem_limit_bytes=60 << 20),
    )(lag_matrix, past_current, excitation, block_inverse)


def solution(mesh):
    in_specs = (P("lag", "row", None), P("lag", None, "row"), P(None, None, "row"), P("row", None, None))
    return jax.shard_map(per_device, mesh=mesh, in_specs=in_specs, out_specs=P(None, "lag", "row"), check_vma=False)
```

```python
import jax
import jax.numpy as jnp
from jax import lax
from jax.experimental import pallas as pl
from jax.experimental.pallas import tpu as pltpu
from jax.sharding import PartitionSpec as P

MESH = pl.DeviceIdType.MESH
NT = (((1,), (1,)), ((), ()))
F32 = jnp.float32
CHIPS = [(1, 0), (1, 1), (3, 0), (3, 1), (2, 0), (2, 1), (0, 1), (0, 0)]


def kernel(m_hbm, p_hbm, e_hbm, b_hbm, out_ref, mv, g, tg, acc, acc2, xbuf, part, rbuf, ex, binv, newest,
           m_sem, loc_sem, ga_s, ga_r, gt_s, gt_r, sib_s, sib_r, sh_s, sh_r, x_s, x_r, rs_s, rs_r, nb_s, nb_r):
    lag, row = lax.axis_index("lag"), lax.axis_index("row")
    core, x, zl = lag % 2, (lag // 2) % 4, lag // 8
    chip = lag // 2
    y, h = row // 2, row % 2
    yp, ym, y2, ho = (y + 1) % 4, (y + 3) % 4, (y + 2) % 4, 1 - h
    W = p_hbm.shape[-1]
    S = ex.shape[1]
    older = (core == 0) & (lag > 0)

    shards = [y * 2 + h, ym * 2 + h, yp * 2 + h, y * 2 + ho, y2 * 2 + h, ym * 2 + ho, yp * 2 + ho, y2 * 2 + ho]
    sibling = lag + 1 - 2 * core
    elder = (lag + 1) % 16
    peers = [(((zl + dz) % 2) * 4 + (x + dx) % 4) for dx, dz in CHIPS]
    peer_lags = [p * 2 + core for p in peers]

    barrier = pltpu.get_barrier_semaphore()
    for k in (1, 2, 3):
        pl.semaphore_signal(barrier, 1, device_id={"row": shards[k]}, device_id_type=MESH)
    for k in range(1, 16):
        pl.semaphore_signal(barrier, 1, device_id={"lag": (lag + k) % 16}, device_id_type=MESH)

    loads = [pltpu.make_async_copy(p_hbm.at[:, c], g.at[c, row], loc_sem.at[c]) for c in range(2)]
    loads += [pltpu.make_async_copy(e_hbm.at[:, pl.ds(pl.multiple_of(lag * S, S), S)], ex, loc_sem.at[2]),
              pltpu.make_async_copy(b_hbm, binv, loc_sem.at[3])]
    m_loads = [pltpu.make_async_copy(m_hbm.at[0, :, pl.ds(pl.multiple_of(s * W, W), W)], mv.at[s], m_sem.at[k])
               for k, s in enumerate(shards)]
    for cp in loads[:2] + m_loads + loads[2:]:
        cp.start()
    loads[0].wait()
    loads[1].wait()
    pl.semaphore_wait(barrier, 18)

    def mm(dst, src, s, first):
        v_rows = src.shape[1] * src.shape[2]

        @pl.loop(0, 4)
        def _(n):
            cols = pl.ds(pl.multiple_of(n * (W // 4), W // 4), W // 4)
            v = lax.dot_general(src[s].reshape(v_rows, W), mv[s, cols, :], NT, preferred_element_type=F32)
            v = v.reshape(src.shape[1], src.shape[2], W // 4)
            if first:
                dst[:, :, cols] = v
            else:
                dst[:, :, cols] += v

    class Gather:
        SENDS = [(0, "0", 2), (0, "0", 1), (1, "0a", 2), (2, "0b", 1), (0, "0", 3), (1, "0", 3), (2, "0", 3), (4, "0a", 3),
                 (4, "0b", 3), (0, "1", 2), (0, "1", 1), (1, "1a", 2), (2, "1b", 1), (0, "1", 3), (3, "1", 2), (3, "1", 1),
                 (5, "1a", 2), (6, "1b", 1)]
        ARRIVE = [(1, "0"), (2, "0"), (4, "0a"), (4, "0b"), (3, "0"), (5, "0"), (6, "0"), (7, "0a"), (7, "0b"), (1, "1"),
                  (2, "1"), (4, "1a"), (4, "1b"), (3, "1"), (5, "1"), (6, "1"), (7, "1a"), (7, "1b")]

        def __init__(self, buf, c, ss, rs, split):
            self.buf, self.c, self.ss, self.rs = buf, c, ss, rs
            a, n = split // 2, 8 - split
            self.blocks = {"0": (0, split), "0a": (0, a), "0b": (a, split - a),
                           "1": (split, n), "1a": (split, n // 2), "1b": (split + n // 2, n - n // 2)}

        def copy(self, i, k, blocks, to):
            lo, n = self.blocks[blocks]
            ref = self.buf.at[self.c, shards[k], pl.ds(lo, n)]
            return pltpu.make_async_remote_copy(ref, ref, self.ss.at[self.c, i], self.rs.at[self.c, i],
                                                device_id={"row": shards[to]}, device_id_type=MESH)

        def start(self, *which):
            for i in which:
                self.copy(i, *self.SENDS[i]).start()

        def wait(self, *which):
            for i in which:
                k, blocks = self.ARRIVE[i]
                self.copy(i, k, blocks, self.SENDS[i][2]).wait_recv()

        def drain(self):
            for i in range(18):
                self.copy(i, *self.SENDS[i]).wait_send()

        def own(self):
            self.start(13, 0, 1, 9, 10, 4)

        def relay1(self, on_shard):
            self.wait(13)
            self.start(14, 15)
            self.wait(0)
            self.start(2, 5)
            self.wait(1)
            self.start(3, 6)
            self.wait(9)
            self.start(11)
            on_shard(1)
            self.wait(10)
            self.start(12)
            on_shard(2)

        def relay2(self, on_shard):
            self.wait(4)
            on_shard(3)
            self.wait(2)
            self.start(7)
            self.wait(3)
            self.start(8)
            self.wait(14)
            self.start(16)
            self.wait(15)
            self.start(17)

        def rest(self, on_shard):
            self.wait(11, 12)
            on_shard(4)
            self.wait(5)
            on_shard(5)
            self.wait(6)
            on_shard(6)
            self.wait(7, 8, 16, 17)
            on_shard(7)

    def sibling_copy(c, k):
        s = shards[k]
        return pltpu.make_async_remote_copy(g.at[c, s], tg.at[c, s], sib_s.at[c, k], sib_r.at[c, k],
                                            device_id={"lag": sibling}, device_id_type=MESH)

    shift = [pltpu.make_async_remote_copy(g.at[c, row], tg.at[c, row], sh_s.at[c], sh_r.at[c],
                                          device_id={"lag": elder}, device_id_type=MESH) for c in range(2)]

    def exchange(step, total, c, k):
        return pltpu.make_async_remote_copy(total.at[c, peers[k]], xbuf.at[step, k], x_s.at[step, k], x_r.at[step, k],
                                            device_id={"lag": sibling}, device_id_type=MESH)

    def to_owner(step, k):
        return pltpu.make_async_remote_copy(part.at[step, k], rbuf.at[step, k], rs_s.at[step, k], rs_r.at[step, k],
                                            device_id={"lag": peer_lags[k]}, device_id_type=MESH)

    def hand_over(step, total, c):
        for k in range(8):
            exchange(step, total, c, k).start()

    def reduce_send(step, total, c):
        for k in range(8):
            exchange(step, total, c, k).wait_recv()
            part[step, k] = total[c, peers[k]] + xbuf[step, k]
            if k < 7:
                to_owner(step, k).start()

    def finish(step):
        history = part[step, 7]
        for k in range(7):
            to_owner(step, k).wait_recv()
            history = history + rbuf[step, k]
        source = ex[step] - history
        for b in range(binv.shape[0]):
            v = lax.dot_general(source[:, b * 128:(b + 1) * 128], binv[b], NT, precision=lax.Precision.HIGHEST,
                                preferred_element_type=F32)
            newest[step, :, pl.ds(b * 128, 128)] = v.astype(newest.dtype)
        out_ref[step] = newest[step]

    def to_first(c):
        return pltpu.make_async_remote_copy(newest.at[0], tg.at[c, row, chip], nb_s.at[0], nb_r.at[lag],
                                            device_id={"lag": 0}, device_id_type=MESH)

    def from_lag(c, k):
        ref = tg.at[c, row, k]
        return pltpu.make_async_remote_copy(ref, ref, nb_s.at[0], nb_r.at[2 * k + c], device_id={"lag": 0}, device_id_type=MESH)

    def a_shard(c):
        def on_shard(k):
            @pl.when(core == 0)
            def _():
                sibling_copy(c, k).start()
            if c == 0:
                m_loads[k].wait()
            mm(acc.at[c], g.at[c], shards[k], k == 0)
        return on_shard

    def t_shard(c):
        return lambda k: mm(acc2.at[c], tg.at[c], shards[k], k == 0)

    a = [Gather(g, c, ga_s, ga_r, 4 - c) for c in range(2)]
    t = [Gather(tg, c, gt_s, gt_r, 4 - c) for c in range(2)]

    a[0].own()

    @pl.when((core == 1) & (lag < 15))
    def _():
        shift[0].start()
        shift[1].start()
    a_shard(0)(0)
    a[0].relay1(a_shard(0))
    a[1].own()
    a[0].relay2(a_shard(0))
    a_shard(1)(0)
    a[0].rest(a_shard(0))

    @pl.when(core == 1)
    def _():
        hand_over(0, acc, 0)

    @pl.when(core == 0)
    def _():
        reduce_send(0, acc, 0)
    a[1].relay1(a_shard(1))
    a[1].relay2(a_shard(1))
    loads[2].wait()
    loads[3].wait()

    @pl.when(core == 0)
    def _():
        finish(0)

    @pl.when(lag == 0)
    def _():
        tg[0, row, 0] = newest[0]

    @pl.when(older)
    def _():
        to_first(0).start()
        shift[0].wait_recv()
        shift[1].wait_recv()
        t[0].own()
    a[1].rest(a_shard(1))

    @pl.when(core == 0)
    def _():
        hand_over(0, acc, 1)

    @pl.when(core == 1)
    def _():
        reduce_send(0, acc, 1)
        for k in range(8):
            sibling_copy(0, k).wait_recv()
            t_shard(0)(k)
        hand_over(1, acc2, 0)
        finish(0)
        to_first(1).start()
        for k in range(8):
            sibling_copy(1, k).wait_recv()
            t_shard(1)(k)
        reduce_send(1, acc2, 1)

    @pl.when(older)
    def _():
        t_shard(0)(0)
        t[0].relay1(t_shard(0))
        t[1].own()
        t[0].relay2(t_shard(0))
        t_shard(1)(0)
        t[0].rest(t_shard(0))
        reduce_send(1, acc2, 0)
        t[1].relay1(t_shard(1))
        t[1].relay2(t_shard(1))
        t[1].rest(t_shard(1))
        hand_over(1, acc2, 1)

    @pl.when(lag == 0)
    def _():
        for k in range(1, 8):
            from_lag(0, k).wait_recv()
        t[0].own()
        t_shard(0)(0)
        t[0].relay1(t_shard(0))
        t[0].relay2(t_shard(0))
        t[0].rest(t_shard(0))
        reduce_send(1, acc2, 0)
        for k in range(8):
            from_lag(1, k).wait_recv()
        t[1].own()
        t_shard(1)(0)
        t[1].relay1(t_shard(1))
        t[1].relay2(t_shard(1))
        t[1].rest(t_shard(1))
        hand_over(1, acc2, 1)

    finish(1)

    a[0].drain()
    a[1].drain()
    for k in range(7):
        to_owner(0, k).wait_send()
        to_owner(1, k).wait_send()

    @pl.when(core == 0)
    def _():
        t[0].drain()
        t[1].drain()
        for k in range(8):
            for c in range(2):
                sibling_copy(c, k).wait_send()
                exchange(c, (acc, acc2)[c], 1, k).wait_send()

    @pl.when(lag > 0)
    def _():
        to_first(0).wait_send()

    @pl.when(core == 1)
    def _():
        for k in range(8):
            for step in range(2):
                exchange(step, (acc, acc2)[step], 0, k).wait_send()

    @pl.when((core == 1) & (lag < 15))
    def _():
        shift[0].wait_send()
        shift[1].wait_send()


def per_device(lag_matrix, past_current, excitation, block_inverse):
    E, W = past_current.shape[1:]
    S = E // 16
    nb = block_inverse.shape[0]
    bf = past_current.dtype
    dma = pltpu.SemaphoreType.DMA
    past = past_current.reshape(8, 2, S, W)
    return pl.pallas_call(
        kernel,
        out_shape=jax.ShapeDtypeStruct((2, S, W), bf),
        in_specs=[pl.BlockSpec(memory_space=pl.ANY)] * 4,
        out_specs=pl.BlockSpec(memory_space=pltpu.VMEM),
        scratch_shapes=[
            pltpu.VMEM((8, W, W), bf), pltpu.VMEM((2, 8, 8, S, W), bf), pltpu.VMEM((2, 8, 8, S, W), bf),
            pltpu.VMEM((2, 8, S, W), F32), pltpu.VMEM((2, 8, S, W), F32),
            pltpu.VMEM((2, 8, S, W), F32), pltpu.VMEM((2, 8, S, W), F32), pltpu.VMEM((2, 7, S, W), F32),
            pltpu.VMEM((2, S, W), F32), pltpu.VMEM((nb, 128, 128), F32), pltpu.VMEM((2, S, W), bf),
            dma((8,)), dma((4,)), dma((2, 18)), dma((2, 18)), dma((2, 18)), dma((2, 18)), dma((2, 8)), dma((2, 8)),
            dma((2,)), dma((2,)), dma((2, 8)), dma((2, 8)), dma((2, 7)), dma((2, 7)), dma((1,)), dma((16,)),
        ],
        compiler_params=pltpu.CompilerParams(collective_id=0, has_side_effects=True, vmem_limit_bytes=60 << 20),
    )(lag_matrix, past, excitation, block_inverse)


def solution(mesh):
    in_specs = (P("lag", "row", None), P("lag", None, "row"), P(None, None, "row"), P("row", None, None))
    return jax.shard_map(per_device, mesh=mesh, in_specs=in_specs, out_specs=P(None, "lag", "row"), check_vma=False)
```

```python
import jax
import jax.numpy as jnp
from jax import lax
from jax.experimental import pallas as pl
from jax.experimental.pallas import tpu as pltpu
from jax.sharding import PartitionSpec as P

MESH = pl.DeviceIdType.MESH
NT = (((1,), (1,)), ((), ()))
F32 = jnp.float32
CHIPS = [(1, 0), (1, 1), (3, 0), (3, 1), (2, 0), (2, 1), (0, 1), (0, 0)]


def kernel(m_hbm, p_hbm, e_hbm, b_hbm, out_ref, mv, g, tg, acc, acc2, xbuf, part, rbuf, ex, binv, newest,
           m_sem, loc_sem, ga_s, ga_r, gt_s, gt_r, sib_s, sib_r, sh_s, sh_r, x_s, x_r, rs_s, rs_r, nb_s, nb_r, passed, pn_s, pn_r):
    lag, row = lax.axis_index("lag"), lax.axis_index("row")
    core, x, zl = lag % 2, (lag // 2) % 4, lag // 8
    y, h = row // 2, row % 2
    yp, ym, y2, ho = (y + 1) % 4, (y + 3) % 4, (y + 2) % 4, 1 - h
    W = p_hbm.shape[-1]
    S = ex.shape[1]
    older = (core == 0) & (lag > 0)

    shards = [y * 2 + h, ym * 2 + h, yp * 2 + h, y * 2 + ho, y2 * 2 + h, ym * 2 + ho, yp * 2 + ho, y2 * 2 + ho]
    sibling = lag + 1 - 2 * core
    elder = (lag + 1) % 16
    peers = [(((zl + dz) % 2) * 4 + (x + dx) % 4) for dx, dz in CHIPS]
    peer_lags = [p * 2 + core for p in peers]

    barrier = pltpu.get_barrier_semaphore()
    for k in (1, 2, 3):
        pl.semaphore_signal(barrier, 1, device_id={"row": shards[k]}, device_id_type=MESH)
    for k in range(1, 16):
        pl.semaphore_signal(barrier, 1, device_id={"lag": (lag + k) % 16}, device_id_type=MESH)

    loads = [pltpu.make_async_copy(p_hbm, g.at[row], loc_sem.at[0]),
             pltpu.make_async_copy(e_hbm.at[:, pl.ds(pl.multiple_of(lag * S, S), S)], ex, loc_sem.at[1]),
             pltpu.make_async_copy(b_hbm, binv, loc_sem.at[2])]
    m_loads = [pltpu.make_async_copy(m_hbm.at[0, :, pl.ds(pl.multiple_of(s * W, W), W)], mv.at[s], m_sem.at[k])
               for k, s in enumerate(shards)]
    for cp in loads[:1] + m_loads + loads[1:]:
        cp.start()
    loads[0].wait()
    pl.semaphore_wait(barrier, 18)

    def mm(dst, src, s, first):
        v_rows = src.shape[0] * src.shape[1]

        @pl.loop(0, 4)
        def _(n):
            cols = pl.ds(pl.multiple_of(n * (W // 4), W // 4), W // 4)
            v = lax.dot_general(src[...].reshape(v_rows, W), mv[s, cols, :], NT, preferred_element_type=F32)
            v = v.reshape(src.shape[0], src.shape[1], W // 4)
            if first:
                dst[:, :, cols] = v
            else:
                dst[:, :, cols] += v

    class Gather:
        SENDS = [(0, "0", 2), (0, "0", 1), (1, "0a", 2), (2, "0b", 1), (0, "0", 3), (1, "0", 3), (2, "0", 3), (4, "0a", 3),
                 (4, "0b", 3), (0, "1", 2), (0, "1", 1), (1, "1a", 2), (2, "1b", 1), (0, "1", 3), (3, "1", 2), (3, "1", 1),
                 (5, "1a", 2), (6, "1b", 1)]
        ARRIVE = [(1, "0"), (2, "0"), (4, "0a"), (4, "0b"), (3, "0"), (5, "0"), (6, "0"), (7, "0a"), (7, "0b"), (1, "1"),
                  (2, "1"), (4, "1a"), (4, "1b"), (3, "1"), (5, "1"), (6, "1"), (7, "1a"), (7, "1b")]

        def __init__(self, shard, total, ss, rs, split):
            self.shard, self.ss, self.rs = shard, ss, rs
            a, n = split // 2, total - split
            self.blocks = {"0": (0, split), "0a": (0, a), "0b": (a, split - a),
                           "1": (split, n), "1a": (split, n // 2), "1b": (split + n // 2, n - n // 2)}

        def copy(self, i, k, blocks, to):
            lo, n = self.blocks[blocks]
            ref = self.shard(shards[k]).at[pl.ds(lo, n)]
            return pltpu.make_async_remote_copy(ref, ref, self.ss.at[i], self.rs.at[i],
                                                device_id={"row": shards[to]}, device_id_type=MESH)

        def start(self, *which):
            for i in self.used(which):
                self.copy(i, *self.SENDS[i]).start()

        def used(self, which):
            return [i for i in which if self.blocks[self.SENDS[i][1]][1]]

        def wait(self, *which):
            for i in self.used(which):
                k, blocks = self.ARRIVE[i]
                self.copy(i, k, blocks, self.SENDS[i][2]).wait_recv()

        def drain(self):
            for i in self.used(range(18)):
                self.copy(i, *self.SENDS[i]).wait_send()

        def own(self):
            self.start(13, 0, 1, 9, 10, 4)

        def relay1(self):
            self.wait(13)
            self.start(14, 15)
            self.wait(0)
            self.start(2, 5)
            self.wait(1)
            self.start(3, 6)
            self.wait(9)
            self.start(11)
            self.wait(10)
            self.start(12)

        def relay2(self):
            self.wait(2)
            self.start(7)
            self.wait(3)
            self.start(8)
            self.wait(14)
            self.start(16)
            self.wait(15)
            self.start(17)

        def rest(self, on_shard):
            self.wait(5)
            on_shard(5)
            self.wait(6)
            on_shard(6)
            self.wait(7, 8, 16, 17)
            on_shard(7)

    def sibling_copy(k):
        ref = g.at[shards[k]]
        return pltpu.make_async_remote_copy(ref, tg.at[shards[k]], sib_s.at[k], sib_r.at[k],
                                            device_id={"lag": sibling}, device_id_type=MESH)

    shift = pltpu.make_async_remote_copy(g.at[row], tg.at[row], sh_s.at[0], sh_r.at[0],
                                         device_id={"lag": elder}, device_id_type=MESH)

    def exchange(step, k):
        return pltpu.make_async_remote_copy((acc, acc2)[step].at[peers[k] * 2 + 1 - core], xbuf.at[step, k], x_s.at[step, k],
                                            x_r.at[step, k], device_id={"lag": sibling}, device_id_type=MESH)

    def to_owner(step, k):
        return pltpu.make_async_remote_copy(part.at[step, k], rbuf.at[step, k], rs_s.at[step, k], rs_r.at[step, k],
                                            device_id={"lag": peer_lags[k]}, device_id_type=MESH)

    def reduce_send(step):
        for k in range(8):
            exchange(step, k).start()
        for k in range(8):
            exchange(step, k).wait_recv()
            part[step, k] = (acc, acc2)[step][peer_lags[k]] + xbuf[step, k]
            if k < 7:
                to_owner(step, k).start()

    def finish(step):
        history = part[step, 7]
        for k in range(7):
            to_owner(step, k).wait_recv()
            history = history + rbuf[step, k]
        source = ex[step] - history
        for b in range(binv.shape[0]):
            v = lax.dot_general(source[:, b * 128:(b + 1) * 128], binv[b], NT, precision=lax.Precision.HIGHEST,
                                preferred_element_type=F32)
            newest[step, :, pl.ds(b * 128, 128)] = v.astype(newest.dtype)
        out_ref[step] = newest[step]

    near, far = (0, 1, 2, 4), (3, 5, 6, 7)
    partner = pltpu.make_async_remote_copy(newest.at[0], passed, pn_s.at[0], pn_r.at[0],
                                           device_id={"row": shards[3]}, device_id_type=MESH)

    def to_first(k, owner=0):
        return pltpu.make_async_remote_copy(passed if owner else newest.at[0], tg.at[shards[owner], lag],
                                            nb_s.at[k + (owner > 0) * 8], nb_r.at[shards[owner]],
                                            device_id={"lag": 0, "row": shards[k]}, device_id_type=MESH)

    def to_first_own(act):
        for k in near[1:]:
            act(to_first(k))

        @pl.when(lag > 0)
        def _():
            act(to_first(0))

        @pl.when(zl == 1)
        def _():
            for k in far:
                act(to_first(k))

    def to_first_passed(act):
        @pl.when(zl == 0)
        def _():
            for k in near[1:]:
                act(to_first(k, 3))

        @pl.when((zl == 0) & (lag > 0))
        def _():
            act(to_first(0, 3))

    def first_wait(k):
        ref = tg.at[shards[k], pl.ds(1, 15)] if k in (0, 3) else tg.at[shards[k]]
        pltpu.make_async_remote_copy(ref, ref, nb_s.at[0], nb_r.at[shards[k]], device_id={"lag": 1},
                                     device_id_type=MESH).wait_recv()

    def a_shard(k):
        m_loads[k].wait()
        mm(acc, g.at[shards[k]], shards[k], k == 0)

    def t_shard(k):
        mm(acc2, tg.at[shards[k]], shards[k], k == 0)

    a = Gather(lambda s: g.at[s], 16, ga_s, ga_r, 7)
    t = Gather(lambda s: tg.at[s], 16, gt_s, gt_r, 7)

    a.own()

    @pl.when((core == 1) & (lag < 15))
    def _():
        shift.start()
    a_shard(0)
    a.relay1()
    a_shard(1)
    a.relay2()
    a_shard(2)
    a.wait(4)
    a_shard(3)
    a.wait(11, 12)
    a_shard(4)
    a.rest(a_shard)
    reduce_send(0)

    @pl.when(core == 0)
    def _():
        for k in range(8):
            sibling_copy(k).start()

    @pl.when(older)
    def _():
        shift.wait_recv()
        t.own()
    loads[1].wait()
    loads[2].wait()
    finish(0)

    @pl.when(zl == 0)
    def _():
        partner.start()
    to_first_own(lambda cp: cp.start())

    @pl.when(zl == 0)
    def _():
        partner.wait_recv()
    to_first_passed(lambda cp: cp.start())

    @pl.when(core == 1)
    def _():
        for k in range(8):
            sibling_copy(k).wait_recv()
            t_shard(k)

    @pl.when(older)
    def _():
        t_shard(0)
        t.relay1()
        t_shard(1)
        t.relay2()
        t_shard(2)
        t.wait(4)
        t_shard(3)
        t.wait(11, 12)
        t_shard(4)
        t.rest(t_shard)

    @pl.when(lag == 0)
    def _():
        tg[row, 0] = newest[0]
        tg[shards[3], 0] = passed[...]
        for n, k in enumerate(near + far):
            first_wait(k)
            mm(acc2, tg.at[shards[k]], shards[k], n == 0)

    reduce_send(1)
    finish(1)

    a.drain()
    for step in range(2):
        for k in range(8):
            exchange(step, k).wait_send()
        for k in range(7):
            to_owner(step, k).wait_send()
    to_first_own(lambda cp: cp.wait_send())
    to_first_passed(lambda cp: cp.wait_send())

    @pl.when(zl == 0)
    def _():
        partner.wait_send()

    @pl.when(older)
    def _():
        t.drain()

    @pl.when(core == 0)
    def _():
        for k in range(8):
            sibling_copy(k).wait_send()

    @pl.when((core == 1) & (lag < 15))
    def _():
        shift.wait_send()


def per_device(lag_matrix, past_current, excitation, block_inverse):
    E, W = past_current.shape[1:]
    S = E // 16
    nb = block_inverse.shape[0]
    bf = past_current.dtype
    dma = pltpu.SemaphoreType.DMA
    past = past_current.reshape(16, S, W)
    return pl.pallas_call(
        kernel,
        out_shape=jax.ShapeDtypeStruct((2, S, W), bf),
        in_specs=[pl.BlockSpec(memory_space=pl.ANY)] * 4,
        out_specs=pl.BlockSpec(memory_space=pltpu.VMEM),
        scratch_shapes=[
            pltpu.VMEM((8, W, W), bf), pltpu.VMEM((8, 16, S, W), bf), pltpu.VMEM((8, 16, S, W), bf),
            pltpu.VMEM((16, S, W), F32), pltpu.VMEM((16, S, W), F32),
            pltpu.VMEM((2, 8, S, W), F32), pltpu.VMEM((2, 8, S, W), F32), pltpu.VMEM((2, 7, S, W), F32),
            pltpu.VMEM((2, S, W), F32), pltpu.VMEM((nb, 128, 128), F32), pltpu.VMEM((2, S, W), bf),
            dma((8,)), dma((3,)), dma((18,)), dma((18,)), dma((18,)), dma((18,)), dma((8,)), dma((8,)),
            dma((1,)), dma((1,)), dma((2, 8)), dma((2, 8)), dma((2, 7)), dma((2, 7)), dma((16,)), dma((8,)),
            pltpu.VMEM((S, W), bf), dma((1,)), dma((1,)),
        ],
        compiler_params=pltpu.CompilerParams(collective_id=0, has_side_effects=True, vmem_limit_bytes=60 << 20),
    )(lag_matrix, past, excitation, block_inverse)


def solution(mesh):
    in_specs = (P("lag", "row", None), P("lag", None, "row"), P(None, None, "row"), P("row", None, None))
    return jax.shard_map(per_device, mesh=mesh, in_specs=in_specs, out_specs=P(None, "lag", "row"), check_vma=False)
```

```python
import jax
import jax.numpy as jnp
from jax import lax
from jax.experimental import pallas as pl
from jax.experimental.pallas import tpu as pltpu
from jax.sharding import PartitionSpec as P

MESH = pl.DeviceIdType.MESH
NT = (((1,), (1,)), ((), ()))
F32 = jnp.float32
CHIPS = [(1, 0), (1, 1), (3, 0), (3, 1), (2, 0), (2, 1), (0, 1), (0, 0)]


def kernel(m_hbm, p_hbm, e_hbm, b_hbm, out_ref, mv, g, tg, acc, acc2, xbuf, part, rbuf, ex, binv, newest,
           m_sem, loc_sem, ga_s, ga_r, gt_s, gt_r, sib_s, sib_r, sh_s, sh_r, x_s, x_r, rs_s, rs_r, nb_s, nb_r, passed, pn_s, pn_r, tn, mv1, ln_s, ln_r, yb, yb_s, yb_r, b_high, b_low):
    lag, row = lax.axis_index("lag"), lax.axis_index("row")
    core, x, zl = lag % 2, (lag // 2) % 4, lag // 8
    y, h = row // 2, row % 2
    yp, ym, y2, ho = (y + 1) % 4, (y + 3) % 4, (y + 2) % 4, 1 - h
    W = p_hbm.shape[-1]
    S = ex.shape[1]
    older = (core == 0) & (lag > 0)

    shards = [y * 2 + h, ym * 2 + h, yp * 2 + h, y * 2 + ho, y2 * 2 + h, ym * 2 + ho, yp * 2 + ho, y2 * 2 + ho]
    sibling = lag + 1 - 2 * core
    elder = (lag + 1) % 16
    peers = [(((zl + dz) % 2) * 4 + (x + dx) % 4) for dx, dz in CHIPS]
    peer_lags = [p * 2 + core for p in peers]

    barrier = pltpu.get_barrier_semaphore()
    for k in (1, 2, 3):
        pl.semaphore_signal(barrier, 1, device_id={"row": shards[k]}, device_id_type=MESH)
    for k in range(1, 16):
        pl.semaphore_signal(barrier, 1, device_id={"lag": (lag + k) % 16}, device_id_type=MESH)

    loads = [pltpu.make_async_copy(p_hbm, g.at[row], loc_sem.at[0]),
             pltpu.make_async_copy(e_hbm.at[:, pl.ds(pl.multiple_of(lag * S, S), S)], ex, loc_sem.at[1]),
             pltpu.make_async_copy(b_hbm, binv, loc_sem.at[2])]
    m_loads = [pltpu.make_async_copy(m_hbm.at[0, :, pl.ds(pl.multiple_of(s * W, W), W)], mv.at[s], m_sem.at[k])
               for k, s in enumerate(shards)]
    for cp in loads[:1] + m_loads + loads[1:]:
        cp.start()
    loads[0].wait()
    pl.semaphore_wait(barrier, 18)

    def mm(dst, src, s, first, mv=mv):
        v_rows = src.shape[0] * src.shape[1]

        @pl.loop(0, 4)
        def _(n):
            cols = pl.ds(pl.multiple_of(n * (W // 4), W // 4), W // 4)
            v = lax.dot_general(src[...].reshape(v_rows, W), mv[s, cols, :], NT, preferred_element_type=F32)
            v = v.reshape(src.shape[0], src.shape[1], W // 4)
            if first:
                dst[:, :, cols] = v
            else:
                dst[:, :, cols] += v

    class Gather:
        SENDS = [(0, "0", 2), (0, "0", 1), (1, "0a", 2), (2, "0b", 1), (0, "0", 3), (1, "0", 3), (2, "0", 3), (4, "0a", 3),
                 (4, "0b", 3), (0, "1", 2), (0, "1", 1), (1, "1a", 2), (2, "1b", 1), (0, "1", 3), (3, "1", 2), (3, "1", 1),
                 (5, "1a", 2), (6, "1b", 1)]
        ARRIVE = [(1, "0"), (2, "0"), (4, "0a"), (4, "0b"), (3, "0"), (5, "0"), (6, "0"), (7, "0a"), (7, "0b"), (1, "1"),
                  (2, "1"), (4, "1a"), (4, "1b"), (3, "1"), (5, "1"), (6, "1"), (7, "1a"), (7, "1b")]

        def __init__(self, shard, total, ss, rs, split):
            self.shard, self.ss, self.rs = shard, ss, rs
            a, n = split // 2, total - split
            self.blocks = {"0": (0, split), "0a": (0, a), "0b": (a, split - a),
                           "1": (split, n), "1a": (split, n // 2), "1b": (split + n // 2, n - n // 2)}

        def copy(self, i, k, blocks, to):
            lo, n = self.blocks[blocks]
            ref = self.shard(shards[k]).at[pl.ds(lo, n)]
            return pltpu.make_async_remote_copy(ref, ref, self.ss.at[i], self.rs.at[i],
                                                device_id={"row": shards[to]}, device_id_type=MESH)

        def start(self, *which):
            for i in self.used(which):
                self.copy(i, *self.SENDS[i]).start()

        def used(self, which):
            return [i for i in which if self.blocks[self.SENDS[i][1]][1]]

        def wait(self, *which):
            for i in self.used(which):
                k, blocks = self.ARRIVE[i]
                self.copy(i, k, blocks, self.SENDS[i][2]).wait_recv()

        def drain(self):
            for i in self.used(range(18)):
                self.copy(i, *self.SENDS[i]).wait_send()

        def own(self):
            self.start(13, 0, 1, 9, 10, 4)

        def relay1(self):
            self.wait(13)
            self.start(14, 15)
            self.wait(0)
            self.start(2, 5)
            self.wait(1)
            self.start(3, 6)
            self.wait(9)
            self.start(11)
            self.wait(10)
            self.start(12)

        def relay2(self):
            self.wait(2)
            self.start(7)
            self.wait(3)
            self.start(8)
            self.wait(14)
            self.start(16)
            self.wait(15)
            self.start(17)

        def rest(self, on_shard):
            self.wait(5)
            on_shard(5)
            self.wait(6)
            on_shard(6)
            self.wait(7, 8, 16, 17)
            on_shard(7)

    def sibling_copy(k):
        ref = g.at[shards[k]]
        return pltpu.make_async_remote_copy(ref, tg.at[shards[k]], sib_s.at[k], sib_r.at[k],
                                            device_id={"lag": sibling}, device_id_type=MESH)

    shift = pltpu.make_async_remote_copy(g.at[row], tg.at[row], sh_s.at[0], sh_r.at[0],
                                         device_id={"lag": elder}, device_id_type=MESH)

    def exchange(step, k):
        return pltpu.make_async_remote_copy((acc, acc2)[step].at[peers[k] * 2 + 1 - core], xbuf.at[step, k], x_s.at[step, k],
                                            x_r.at[step, k], device_id={"lag": sibling}, device_id_type=MESH)

    def to_owner(step, k):
        return pltpu.make_async_remote_copy(part.at[step, k], rbuf.at[step, k], rs_s.at[step, k], rs_r.at[step, k],
                                            device_id={"lag": peer_lags[k]}, device_id_type=MESH)

    def reduce_send(step):
        for k in range(8):
            exchange(step, k).start()
        for k in range(8):
            exchange(step, k).wait_recv()
            part[step, k] = (acc, acc2)[step][peer_lags[k]] + xbuf[step, k]
            if k < 7:
                to_owner(step, k).start()

    def finish(step):
        history = part[step, 7]
        for k in range(7):
            to_owner(step, k).wait_recv()
            history = history + rbuf[step, k]
        source = ex[step] - history
        high = source.astype(newest.dtype)
        low = (source - high.astype(F32)).astype(newest.dtype)
        both = jnp.concatenate([high, low], axis=0)
        S = high.shape[0]
        for b in range(binv.shape[0]):
            cols = slice(b * 128, (b + 1) * 128)
            v = lax.dot_general(both[:, cols], b_high[b], NT, preferred_element_type=F32)
            w = lax.dot_general(high[:, cols], b_low[b], NT, preferred_element_type=F32)
            newest[step, :, pl.ds(b * 128, 128)] = (v[:S] + (v[S:] + w)).astype(newest.dtype)
        out_ref[step] = newest[step]

    near, far = (0, 1, 2, 4), (3, 5, 6, 7)
    partner = pltpu.make_async_remote_copy(newest.at[0], passed, pn_s.at[0], pn_r.at[0],
                                           device_id={"row": shards[3]}, device_id_type=MESH)

    def to_first(k, owner=0):
        where = (tg.at[row, lag] if k in near and not owner else tn.at[shards[owner] // 2, lag])
        return pltpu.make_async_remote_copy(passed if owner else newest.at[0], where,
                                            nb_s.at[k + (owner > 0) * 8], nb_r.at[shards[owner]],
                                            device_id={"lag": 0 if k in near and not owner else 1, "row": shards[k]},
                                            device_id_type=MESH)

    def along_y(n):
        there = (1, 0, 2)[n]
        return pltpu.make_async_remote_copy(newest.at[0], yb.at[there], yb_s.at[n], yb_r.at[there],
                                            device_id={"row": shards[(1, 2, 4)[n]]}, device_id_type=MESH)

    def to_first_y(n, z):
        owner = shards[(1, 2, 4)[n]]
        return pltpu.make_async_remote_copy(yb.at[n], tn.at[owner // 2, lag] if z else tg.at[owner, lag],
                                            nb_s.at[8 + 4 * z + n], nb_r.at[owner],
                                            device_id={"lag": z, "row": shards[3 * z]}, device_id_type=MESH)

    def to_first_own(act):
        @pl.when(zl == 1)
        def _():
            for n in range(3):
                act(along_y(n))
            act(to_first(0))
            act(to_first(3))

        @pl.when(zl == 0)
        def _():
            for k in near[1:]:
                act(to_first(k))

        @pl.when((zl == 0) & (lag > 0))
        def _():
            act(to_first(0))

    def to_first_passed(act):
        @pl.when(zl == 0)
        def _():
            for k in near[1:]:
                act(to_first(k, 3))

        @pl.when((zl == 0) & (lag != 1))
        def _():
            act(to_first(0, 3))

        @pl.when(zl == 1)
        def _():
            for n in range(3):
                for z in range(2):
                    act(to_first_y(n, z))

    def first_wait(k):
        ref = tg.at[shards[k]] if k in near else tn.at[shards[k] // 2]
        if k in (0, 3):
            ref = ref.at[pl.ds(1, 15)]
        pltpu.make_async_remote_copy(ref, ref, nb_s.at[0], nb_r.at[shards[k]], device_id={"lag": 2},
                                     device_id_type=MESH).wait_recv()

    def lend(n):
        k = far[n]
        return pltpu.make_async_remote_copy(mv.at[shards[k]], mv1.at[shards[k] // 2], ln_s.at[n], ln_r.at[n],
                                            device_id={"lag": 1}, device_id_type=MESH)

    def a_shard(k):
        m_loads[k].wait()
        mm(acc, g.at[shards[k]], shards[k], k == 0)

    def t_shard(k):
        mm(acc2, tg.at[shards[k]], shards[k], k == 0)

    a = Gather(lambda s: g.at[s], 16, ga_s, ga_r, 7)
    t = Gather(lambda s: tg.at[s], 16, gt_s, gt_r, 7)

    a.own()

    @pl.when((core == 1) & (lag < 15) & (lag != 7))
    def _():
        shift.start()
    a_shard(0)
    loads[1].wait()
    loads[2].wait()
    b_high[...] = binv[...].astype(b_high.dtype)
    b_low[...] = (binv[...] - b_high[...].astype(F32)).astype(b_low.dtype)
    a.relay1()
    a_shard(1)
    a.relay2()
    @pl.when(lag == 7)
    def _():
        shift.start()
    a_shard(2)
    a.wait(4)
    a_shard(3)
    a.wait(11, 12)
    a_shard(4)
    a.rest(a_shard)
    reduce_send(0)

    @pl.when(core == 0)
    def _():
        for k in range(8):
            sibling_copy(k).start()

    @pl.when(lag == 0)
    def _():
        for n in range(4):
            lend(n).start()

    @pl.when(older)
    def _():
        shift.wait_recv()
        t.own()
    finish(0)

    @pl.when(zl == 0)
    def _():
        partner.start()
    to_first_own(lambda cp: cp.start())

    @pl.when(zl == 0)
    def _():
        partner.wait_recv()

    @pl.when(zl == 1)
    def _():
        for n in range(3):
            ref = yb.at[n]
            pltpu.make_async_remote_copy(ref, ref, yb_s.at[n], yb_r.at[n], device_id={"lag": 2}, device_id_type=MESH).wait_recv()
    to_first_passed(lambda cp: cp.start())

    @pl.when(core == 1)
    def _():
        for k in range(8):
            sibling_copy(k).wait_recv()
            t_shard(k)

    @pl.when(older)
    def _():
        t_shard(0)
        t.relay1()
        t_shard(1)
        t.relay2()
        t_shard(2)
        t.wait(4)
        t_shard(3)
        t.wait(11, 12)
        t_shard(4)
        t.rest(t_shard)

    @pl.when(lag == 0)
    def _():
        tg[row, 0] = newest[0]
        for n, k in enumerate(near):
            first_wait(k)
            mm(acc2, tg.at[shards[k]], shards[k], n == 0)

    @pl.when(lag == 1)
    def _():
        tn[y, 1] = passed[...]
        for n, k in enumerate(far):
            lend(n).wait_recv()
            first_wait(k)
            mm(acc2, tn.at[shards[k] // 2], shards[k] // 2, False, mv1)

    reduce_send(1)
    finish(1)

    a.drain()
    for step in range(2):
        for k in range(8):
            exchange(step, k).wait_send()
        for k in range(7):
            to_owner(step, k).wait_send()
    to_first_own(lambda cp: cp.wait_send())
    to_first_passed(lambda cp: cp.wait_send())

    @pl.when(zl == 0)
    def _():
        partner.wait_send()

    @pl.when(lag == 0)
    def _():
        for n in range(4):
            lend(n).wait_send()

    @pl.when(older)
    def _():
        t.drain()

    @pl.when(core == 0)
    def _():
        for k in range(8):
            sibling_copy(k).wait_send()

    @pl.when((core == 1) & (lag < 15))
    def _():
        shift.wait_send()


def per_device(lag_matrix, past_current, excitation, block_inverse):
    E, W = past_current.shape[1:]
    S = E // 16
    nb = block_inverse.shape[0]
    bf = past_current.dtype
    dma = pltpu.SemaphoreType.DMA
    past = past_current.reshape(16, S, W)
    return pl.pallas_call(
        kernel,
        out_shape=jax.ShapeDtypeStruct((2, S, W), bf),
        in_specs=[pl.BlockSpec(memory_space=pl.ANY)] * 4,
        out_specs=pl.BlockSpec(memory_space=pltpu.VMEM),
        scratch_shapes=[
            pltpu.VMEM((8, W, W), bf), pltpu.VMEM((8, 16, S, W), bf), pltpu.VMEM((8, 16, S, W), bf),
            pltpu.VMEM((16, S, W), F32), pltpu.VMEM((16, S, W), F32),
            pltpu.VMEM((2, 8, S, W), F32), pltpu.VMEM((2, 8, S, W), F32), pltpu.VMEM((2, 7, S, W), F32),
            pltpu.VMEM((2, S, W), F32), pltpu.VMEM((nb, 128, 128), F32), pltpu.VMEM((2, S, W), bf),
            dma((8,)), dma((3,)), dma((18,)), dma((18,)), dma((18,)), dma((18,)), dma((8,)), dma((8,)),
            dma((1,)), dma((1,)), dma((2, 8)), dma((2, 8)), dma((2, 7)), dma((2, 7)), dma((16,)), dma((8,)),
            pltpu.VMEM((S, W), bf), dma((1,)), dma((1,)), pltpu.VMEM((4, 16, S, W), bf), pltpu.VMEM((4, W, W), bf), dma((4,)), dma((4,)),
            pltpu.VMEM((3, S, W), bf), dma((3,)), dma((3,)), pltpu.VMEM((nb, 128, 128), bf), pltpu.VMEM((nb, 128, 128), bf),
        ],
        compiler_params=pltpu.CompilerParams(collective_id=0, has_side_effects=True, vmem_limit_bytes=60 << 20),
    )(lag_matrix, past, excitation, block_inverse)


def solution(mesh):
    in_specs = (P("lag", "row", None), P("lag", None, "row"), P(None, None, "row"), P("row", None, None))
    return jax.shard_map(per_device, mesh=mesh, in_specs=in_specs, out_specs=P(None, "lag", "row"), check_vma=False)
```

```python
import jax
import jax.numpy as jnp
from jax import lax
from jax.experimental import pallas as pl
from jax.experimental.pallas import tpu as pltpu
from jax.sharding import PartitionSpec as P

MESH = pl.DeviceIdType.MESH
NT = (((1,), (1,)), ((), ()))
F32 = jnp.float32
CHIPS = [(1, 0), (1, 1), (3, 0), (3, 1), (2, 0), (2, 1), (0, 1), (0, 0)]


def kernel(m_hbm, p_hbm, e_hbm, b_hbm, out_ref, mv, g, tg, acc, acc2, xbuf, part, rbuf, ex, binv, newest,
           m_sem, loc_sem, ga_s, ga_r, gt_s, gt_r, sib_s, sib_r, sh_s, sh_r, x_s, x_r, rs_s, rs_r, nb_s, nb_r, passed, pn_s, pn_r, tn, mv1, ln_s, ln_r, yb, yb_s, yb_r, b_high, b_low):
    lag, row = lax.axis_index("lag"), lax.axis_index("row")
    core, x, zl = lag % 2, (lag // 2) % 4, lag // 8
    y, h = row // 2, row % 2
    yp, ym, y2, ho = (y + 1) % 4, (y + 3) % 4, (y + 2) % 4, 1 - h
    W = p_hbm.shape[-1]
    S = ex.shape[1]
    older = (core == 0) & (lag > 0)

    shards = [y * 2 + h, ym * 2 + h, yp * 2 + h, y * 2 + ho, y2 * 2 + h, ym * 2 + ho, yp * 2 + ho, y2 * 2 + ho]
    sibling = lag + 1 - 2 * core
    elder = (lag + 1) % 16
    peers = [(((zl + dz) % 2) * 4 + (x + dx) % 4) for dx, dz in CHIPS]
    peer_lags = [p * 2 + core for p in peers]

    barrier = pltpu.get_barrier_semaphore()
    for k in (1, 2, 3):
        pl.semaphore_signal(barrier, 1, device_id={"row": shards[k]}, device_id_type=MESH)
    for k in range(1, 16):
        pl.semaphore_signal(barrier, 1, device_id={"lag": (lag + k) % 16}, device_id_type=MESH)

    loads = [pltpu.make_async_copy(p_hbm, g.at[row], loc_sem.at[0]),
             pltpu.make_async_copy(e_hbm.at[:, pl.ds(pl.multiple_of(lag * S, S), S)], ex, loc_sem.at[1]),
             pltpu.make_async_copy(b_hbm, binv, loc_sem.at[2])]
    m_loads = [pltpu.make_async_copy(m_hbm.at[0, :, pl.ds(pl.multiple_of(s * W, W), W)], mv.at[s], m_sem.at[k])
               for k, s in enumerate(shards)]
    for cp in loads[:1] + m_loads + loads[1:]:
        cp.start()
    loads[0].wait()
    pl.semaphore_wait(barrier, 18)

    def mm(dst, src, s, first, mv=mv):
        v_rows = src.shape[0] * src.shape[1]

        @pl.loop(0, 4)
        def _(n):
            cols = pl.ds(pl.multiple_of(n * (W // 4), W // 4), W // 4)
            v = lax.dot_general(src[...].reshape(v_rows, W), mv[s, cols, :], NT, preferred_element_type=F32)
            v = v.reshape(src.shape[0], src.shape[1], W // 4)
            if first:
                dst[:, :, cols] = v
            else:
                dst[:, :, cols] += v

    class Gather:
        SENDS = [(0, "0", 2), (0, "0", 1), (1, "0a", 2), (2, "0b", 1), (0, "0", 3), (1, "0", 3), (2, "0", 3), (4, "0a", 3),
                 (4, "0b", 3), (0, "1", 2), (0, "1", 1), (1, "1a", 2), (2, "1b", 1), (0, "1", 3), (3, "1", 2), (3, "1", 1),
                 (5, "1a", 2), (6, "1b", 1)]
        ARRIVE = [(1, "0"), (2, "0"), (4, "0a"), (4, "0b"), (3, "0"), (5, "0"), (6, "0"), (7, "0a"), (7, "0b"), (1, "1"),
                  (2, "1"), (4, "1a"), (4, "1b"), (3, "1"), (5, "1"), (6, "1"), (7, "1a"), (7, "1b")]

        def __init__(self, shard, total, ss, rs, split):
            self.shard, self.ss, self.rs = shard, ss, rs
            a, n = split // 2, total - split
            self.blocks = {"0": (0, split), "0a": (0, a), "0b": (a, split - a),
                           "1": (split, n), "1a": (split, n // 2), "1b": (split + n // 2, n - n // 2)}

        def copy(self, i, k, blocks, to):
            lo, n = self.blocks[blocks]
            ref = self.shard(shards[k]).at[pl.ds(lo, n)]
            return pltpu.make_async_remote_copy(ref, ref, self.ss.at[i], self.rs.at[i],
                                                device_id={"row": shards[to]}, device_id_type=MESH)

        def start(self, *which):
            for i in self.used(which):
                self.copy(i, *self.SENDS[i]).start()

        def used(self, which):
            return [i for i in which if self.blocks[self.SENDS[i][1]][1]]

        def wait(self, *which):
            for i in self.used(which):
                k, blocks = self.ARRIVE[i]
                self.copy(i, k, blocks, self.SENDS[i][2]).wait_recv()

        def drain(self):
            for i in self.used(range(18)):
                self.copy(i, *self.SENDS[i]).wait_send()

        def own(self):
            self.start(13, 0, 1, 9, 10, 4)

        def relay1(self):
            self.wait(13)
            self.start(14, 15)
            self.wait(0)
            self.start(2, 5)
            self.wait(1)
            self.start(3, 6)
            self.wait(9)
            self.start(11)
            self.wait(10)
            self.start(12)

        def relay2(self):
            self.wait(2)
            self.start(7)
            self.wait(3)
            self.start(8)
            self.wait(14)
            self.start(16)
            self.wait(15)
            self.start(17)

        def rest(self, on_shard):
            self.wait(5)
            on_shard(5)
            self.wait(6)
            on_shard(6)
            self.wait(7, 8, 16, 17)
            on_shard(7)

    def sibling_copy(k):
        ref = g.at[shards[k]]
        return pltpu.make_async_remote_copy(ref, tg.at[shards[k]], sib_s.at[k], sib_r.at[k],
                                            device_id={"lag": sibling}, device_id_type=MESH)

    shift = pltpu.make_async_remote_copy(g.at[row], tg.at[row], sh_s.at[0], sh_r.at[0],
                                         device_id={"lag": elder}, device_id_type=MESH)

    def exchange(step, k):
        return pltpu.make_async_remote_copy((acc, acc2)[step].at[peers[k] * 2 + 1 - core], xbuf.at[step, k], x_s.at[step, k],
                                            x_r.at[step, k], device_id={"lag": sibling}, device_id_type=MESH)

    def to_owner(step, k):
        return pltpu.make_async_remote_copy(part.at[step, k], rbuf.at[step, k], rs_s.at[step, k], rs_r.at[step, k],
                                            device_id={"lag": peer_lags[k]}, device_id_type=MESH)

    def reduce_send(step):
        for k in range(8):
            exchange(step, k).start()
        for k in range(8):
            exchange(step, k).wait_recv()
            part[step, k] = (acc, acc2)[step][peer_lags[k]] + xbuf[step, k]
            if k < 7:
                to_owner(step, k).start()

    def finish(step):
        history = part[step, 7]
        for k in range(7):
            to_owner(step, k).wait_recv()
            history = history + rbuf[step, k]
        source = ex[step] - history
        high = source.astype(newest.dtype)
        low = (source - high.astype(F32)).astype(newest.dtype)
        both = jnp.concatenate([high, low], axis=0)
        S = high.shape[0]
        for b in range(binv.shape[0]):
            cols = slice(b * 128, (b + 1) * 128)
            v = lax.dot_general(both[:, cols], b_high[b], NT, preferred_element_type=F32)
            w = lax.dot_general(high[:, cols], b_low[b], NT, preferred_element_type=F32)
            newest[step, :, pl.ds(b * 128, 128)] = (v[:S] + (v[S:] + w)).astype(newest.dtype)
        out_ref[step] = newest[step]

    near, far = (0, 1, 2, 4), (3, 5, 6, 7)
    partner = pltpu.make_async_remote_copy(newest.at[0], passed, pn_s.at[0], pn_r.at[0],
                                           device_id={"row": shards[3]}, device_id_type=MESH)

    def to_first(k, owner=0):
        where = (tg.at[row, lag] if k in near and not owner else tn.at[shards[owner] // 2, lag])
        return pltpu.make_async_remote_copy(passed if owner else newest.at[0], where,
                                            nb_s.at[k + (owner > 0) * 8], nb_r.at[shards[owner]],
                                            device_id={"lag": 0 if k in near and not owner else 1, "row": shards[k]},
                                            device_id_type=MESH)

    def along_y(n):
        there = (1, 0, 2)[n]
        return pltpu.make_async_remote_copy(newest.at[0], yb.at[there], yb_s.at[n], yb_r.at[there],
                                            device_id={"row": shards[(1, 2, 4)[n]]}, device_id_type=MESH)

    def to_first_y(n, z):
        owner = shards[(1, 2, 4)[n]]
        return pltpu.make_async_remote_copy(yb.at[n], tn.at[owner // 2, lag] if z else tg.at[owner, lag],
                                            nb_s.at[8 + 4 * z + n], nb_r.at[owner],
                                            device_id={"lag": z, "row": shards[3 * z]}, device_id_type=MESH)

    def to_first_own(act):
        @pl.when(zl == 1)
        def _():
            for n in range(3):
                act(along_y(n))
            act(to_first(0))
            act(to_first(3))

        @pl.when(zl == 0)
        def _():
            for k in near[1:]:
                act(to_first(k))

        @pl.when((zl == 0) & (lag > 0))
        def _():
            act(to_first(0))

    def to_first_passed(act):
        @pl.when(zl == 0)
        def _():
            for k in near[1:]:
                act(to_first(k, 3))

        @pl.when((zl == 0) & (lag != 1))
        def _():
            act(to_first(0, 3))

        @pl.when(zl == 1)
        def _():
            for n in range(3):
                for z in range(2):
                    act(to_first_y(n, z))

    def first_wait(k):
        ref = tg.at[shards[k]] if k in near else tn.at[shards[k] // 2]
        if k in (0, 3):
            ref = ref.at[pl.ds(1, 15)]
        pltpu.make_async_remote_copy(ref, ref, nb_s.at[0], nb_r.at[shards[k]], device_id={"lag": 2},
                                     device_id_type=MESH).wait_recv()

    def lend(n):
        k = far[n]
        return pltpu.make_async_remote_copy(mv.at[shards[k]], mv1.at[shards[k] // 2], ln_s.at[n], ln_r.at[n],
                                            device_id={"lag": 1}, device_id_type=MESH)

    def a_shard(k):
        m_loads[k].wait()
        mm(acc, g.at[shards[k]], shards[k], k == 0)

    def t_shard(k):
        mm(acc2, tg.at[shards[k]], shards[k], k == 0)

    a = Gather(lambda s: g.at[s], 16, ga_s, ga_r, 6)
    t = Gather(lambda s: tg.at[s], 16, gt_s, gt_r, 7)

    a.own()

    @pl.when((core == 1) & (lag < 15) & (lag != 7))
    def _():
        shift.start()
    a_shard(0)
    loads[1].wait()
    loads[2].wait()
    b_high[...] = binv[...].astype(b_high.dtype)
    b_low[...] = (binv[...] - b_high[...].astype(F32)).astype(b_low.dtype)
    a.relay1()
    a_shard(1)
    a.relay2()
    @pl.when(lag == 7)
    def _():
        shift.start()
    a_shard(2)
    a.wait(4)
    a_shard(3)
    a.wait(11, 12)
    a_shard(4)
    a.rest(a_shard)
    reduce_send(0)

    @pl.when(core == 0)
    def _():
        for k in range(8):
            sibling_copy(k).start()

    @pl.when(lag == 0)
    def _():
        for n in range(4):
            lend(n).start()

    @pl.when(older)
    def _():
        shift.wait_recv()
        t.own()
    finish(0)

    @pl.when(zl == 0)
    def _():
        partner.start()
    to_first_own(lambda cp: cp.start())

    @pl.when(zl == 0)
    def _():
        partner.wait_recv()

    @pl.when(zl == 1)
    def _():
        for n in range(3):
            ref = yb.at[n]
            pltpu.make_async_remote_copy(ref, ref, yb_s.at[n], yb_r.at[n], device_id={"lag": 2}, device_id_type=MESH).wait_recv()
    to_first_passed(lambda cp: cp.start())

    @pl.when(core == 1)
    def _():
        for k in range(8):
            sibling_copy(k).wait_recv()
            t_shard(k)

    @pl.when(older)
    def _():
        t_shard(0)
        t.relay1()
        t_shard(1)
        t.relay2()
        t_shard(2)
        t.wait(4)
        t_shard(3)
        t.wait(11, 12)
        t_shard(4)
        t.rest(t_shard)

    @pl.when(lag == 0)
    def _():
        tg[row, 0] = newest[0]
        for n, k in enumerate(near):
            first_wait(k)
            mm(acc2, tg.at[shards[k]], shards[k], n == 0)

    @pl.when(lag == 1)
    def _():
        tn[y, 1] = passed[...]
        for n, k in enumerate(far):
            lend(n).wait_recv()
            first_wait(k)
            mm(acc2, tn.at[shards[k] // 2], shards[k] // 2, False, mv1)

    reduce_send(1)
    finish(1)

    a.drain()
    for step in range(2):
        for k in range(8):
            exchange(step, k).wait_send()
        for k in range(7):
            to_owner(step, k).wait_send()
    to_first_own(lambda cp: cp.wait_send())
    to_first_passed(lambda cp: cp.wait_send())

    @pl.when(zl == 0)
    def _():
        partner.wait_send()

    @pl.when(lag == 0)
    def _():
        for n in range(4):
            lend(n).wait_send()

    @pl.when(older)
    def _():
        t.drain()

    @pl.when(core == 0)
    def _():
        for k in range(8):
            sibling_copy(k).wait_send()

    @pl.when((core == 1) & (lag < 15))
    def _():
        shift.wait_send()


def per_device(lag_matrix, past_current, excitation, block_inverse):
    E, W = past_current.shape[1:]
    S = E // 16
    nb = block_inverse.shape[0]
    bf = past_current.dtype
    dma = pltpu.SemaphoreType.DMA
    past = past_current.reshape(16, S, W)
    return pl.pallas_call(
        kernel,
        out_shape=jax.ShapeDtypeStruct((2, S, W), bf),
        in_specs=[pl.BlockSpec(memory_space=pl.ANY)] * 4,
        out_specs=pl.BlockSpec(memory_space=pltpu.VMEM),
        scratch_shapes=[
            pltpu.VMEM((8, W, W), bf), pltpu.VMEM((8, 16, S, W), bf), pltpu.VMEM((8, 16, S, W), bf),
            pltpu.VMEM((16, S, W), F32), pltpu.VMEM((16, S, W), F32),
            pltpu.VMEM((2, 8, S, W), F32), pltpu.VMEM((2, 8, S, W), F32), pltpu.VMEM((2, 7, S, W), F32),
            pltpu.VMEM((2, S, W), F32), pltpu.VMEM((nb, 128, 128), F32), pltpu.VMEM((2, S, W), bf),
            dma((8,)), dma((3,)), dma((18,)), dma((18,)), dma((18,)), dma((18,)), dma((8,)), dma((8,)),
            dma((1,)), dma((1,)), dma((2, 8)), dma((2, 8)), dma((2, 7)), dma((2, 7)), dma((16,)), dma((8,)),
            pltpu.VMEM((S, W), bf), dma((1,)), dma((1,)), pltpu.VMEM((4, 16, S, W), bf), pltpu.VMEM((4, W, W), bf), dma((4,)), dma((4,)),
            pltpu.VMEM((3, S, W), bf), dma((3,)), dma((3,)), pltpu.VMEM((nb, 128, 128), bf), pltpu.VMEM((nb, 128, 128), bf),
        ],
        compiler_params=pltpu.CompilerParams(collective_id=0, has_side_effects=True, vmem_limit_bytes=60 << 20),
    )(lag_matrix, past, excitation, block_inverse)


def solution(mesh):
    in_specs = (P("lag", "row", None), P("lag", None, "row"), P(None, None, "row"), P("row", None, None))
    return jax.shard_map(per_device, mesh=mesh, in_specs=in_specs, out_specs=P(None, "lag", "row"), check_vma=False)
```

```python
import jax
import jax.numpy as jnp
from jax import lax
from jax.experimental import pallas as pl
from jax.experimental.pallas import tpu as pltpu
from jax.sharding import PartitionSpec as P

MESH = pl.DeviceIdType.MESH
NT = (((1,), (1,)), ((), ()))
F32 = jnp.float32
CHIPS = [(1, 0), (1, 1), (3, 0), (3, 1), (2, 0), (2, 1), (0, 1), (0, 0)]


def kernel(m_hbm, p_hbm, e_hbm, b_hbm, out_ref, mv, g, tg, acc, acc2, xbuf, part, rbuf, ex, binv, newest,
           m_sem, loc_sem, ga_s, ga_r, gt_s, gt_r, sib_s, sib_r, sh_s, sh_r, x_s, x_r, rs_s, rs_r, nb_s, nb_r, passed, pn_s, pn_r, tn, mv1, ln_s, ln_r, yb, yb_s, yb_r, b_high, b_low):
    lag, row = lax.axis_index("lag"), lax.axis_index("row")
    core, x, zl = lag % 2, (lag // 2) % 4, lag // 8
    y, h = row // 2, row % 2
    yp, ym, y2, ho = (y + 1) % 4, (y + 3) % 4, (y + 2) % 4, 1 - h
    W = p_hbm.shape[-1]
    S = ex.shape[1]
    older = (core == 0) & (lag > 0)

    shards = [y * 2 + h, ym * 2 + h, yp * 2 + h, y * 2 + ho, y2 * 2 + h, ym * 2 + ho, yp * 2 + ho, y2 * 2 + ho]
    sibling = lag + 1 - 2 * core
    elder = (lag + 1) % 16
    peers = [(((zl + dz) % 2) * 4 + (x + dx) % 4) for dx, dz in CHIPS]
    peer_lags = [p * 2 + core for p in peers]

    barrier = pltpu.get_barrier_semaphore()
    for k in (1, 2, 3):
        pl.semaphore_signal(barrier, 1, device_id={"row": shards[k]}, device_id_type=MESH)
    for k in range(1, 16):
        pl.semaphore_signal(barrier, 1, device_id={"lag": (lag + k) % 16}, device_id_type=MESH)

    loads = [pltpu.make_async_copy(p_hbm, g.at[row], loc_sem.at[0]),
             pltpu.make_async_copy(e_hbm.at[:, pl.ds(pl.multiple_of(lag * S, S), S)], ex, loc_sem.at[1]),
             pltpu.make_async_copy(b_hbm, binv, loc_sem.at[2])]
    m_loads = [pltpu.make_async_copy(m_hbm.at[0, :, pl.ds(pl.multiple_of(s * W, W), W)], mv.at[s], m_sem.at[k])
               for k, s in enumerate(shards)]
    for cp in loads[:1] + m_loads + loads[1:]:
        cp.start()
    loads[0].wait()
    pl.semaphore_wait(barrier, 18)

    def mm(dst, src, s, first, mv=mv):
        v_rows = src.shape[0] * src.shape[1]

        @pl.loop(0, 4)
        def _(n):
            cols = pl.ds(pl.multiple_of(n * (W // 4), W // 4), W // 4)
            v = lax.dot_general(src[...].reshape(v_rows, W), mv[s, cols, :], NT, preferred_element_type=F32)
            v = v.reshape(src.shape[0], src.shape[1], W // 4)
            if first:
                dst[:, :, cols] = v
            else:
                dst[:, :, cols] += v

    class Gather:
        SENDS = [(0, "0", 2), (0, "0", 1), (1, "0a", 2), (2, "0b", 1), (0, "0", 3), (1, "0", 3), (2, "0", 3), (4, "0a", 3),
                 (4, "0b", 3), (0, "1", 2), (0, "1", 1), (1, "1a", 2), (2, "1b", 1), (0, "1", 3), (3, "1", 2), (3, "1", 1),
                 (5, "1a", 2), (6, "1b", 1)]
        ARRIVE = [(1, "0"), (2, "0"), (4, "0a"), (4, "0b"), (3, "0"), (5, "0"), (6, "0"), (7, "0a"), (7, "0b"), (1, "1"),
                  (2, "1"), (4, "1a"), (4, "1b"), (3, "1"), (5, "1"), (6, "1"), (7, "1a"), (7, "1b")]

        def __init__(self, shard, total, ss, rs, split):
            self.shard, self.ss, self.rs = shard, ss, rs
            a, n = split // 2, total - split
            self.blocks = {"0": (0, split), "0a": (0, a), "0b": (a, split - a),
                           "1": (split, n), "1a": (split, n // 2), "1b": (split + n // 2, n - n // 2)}

        def copy(self, i, k, blocks, to):
            lo, n = self.blocks[blocks]
            ref = self.shard(shards[k]).at[pl.ds(lo, n)]
            return pltpu.make_async_remote_copy(ref, ref, self.ss.at[i], self.rs.at[i],
                                                device_id={"row": shards[to]}, device_id_type=MESH)

        def start(self, *which):
            for i in self.used(which):
                self.copy(i, *self.SENDS[i]).start()

        def used(self, which):
            return [i for i in which if self.blocks[self.SENDS[i][1]][1]]

        def wait(self, *which):
            for i in self.used(which):
                k, blocks = self.ARRIVE[i]
                self.copy(i, k, blocks, self.SENDS[i][2]).wait_recv()

        def drain(self):
            for i in self.used(range(18)):
                self.copy(i, *self.SENDS[i]).wait_send()

        def own(self):
            self.start(13, 0, 1, 9, 10, 4)

        def relay1(self):
            self.wait(13)
            self.start(14, 15)
            self.wait(0)
            self.start(2, 5)
            self.wait(1)
            self.start(3, 6)
            self.wait(9)
            self.start(11)
            self.wait(10)
            self.start(12)

        def relay2(self):
            self.wait(2)
            self.start(7)
            self.wait(3)
            self.start(8)
            self.wait(14)
            self.start(16)
            self.wait(15)
            self.start(17)

        def rest(self, on_shard):
            self.wait(5)
            on_shard(5)
            self.wait(6)
            on_shard(6)
            self.wait(7, 8, 16, 17)
            on_shard(7)

    def sibling_copy(k):
        ref = g.at[shards[k]]
        return pltpu.make_async_remote_copy(ref, tg.at[shards[k]], sib_s.at[k], sib_r.at[k],
                                            device_id={"lag": sibling}, device_id_type=MESH)

    shift = pltpu.make_async_remote_copy(g.at[row], tg.at[row], sh_s.at[0], sh_r.at[0],
                                         device_id={"lag": elder}, device_id_type=MESH)

    def exchange(step, k):
        return pltpu.make_async_remote_copy((acc, acc2)[step].at[peers[k] * 2 + 1 - core], xbuf.at[step, k], x_s.at[step, k],
                                            x_r.at[step, k], device_id={"lag": sibling}, device_id_type=MESH)

    def to_owner(step, k):
        return pltpu.make_async_remote_copy(part.at[step, k], rbuf.at[step, k], rs_s.at[step, k], rs_r.at[step, k],
                                            device_id={"lag": peer_lags[k]}, device_id_type=MESH)

    def reduce_send(step):
        for k in range(8):
            exchange(step, k).start()
        for k in range(8):
            exchange(step, k).wait_recv()
            part[step, k] = (acc, acc2)[step][peer_lags[k]] + xbuf[step, k]
            if k < 7:
                to_owner(step, k).start()

    def finish(step):
        history = part[step, 7]
        for k in range(7):
            to_owner(step, k).wait_recv()
            history = history + rbuf[step, k]
        source = ex[step] - history
        high = source.astype(newest.dtype)
        low = (source - high.astype(F32)).astype(newest.dtype)
        both = jnp.concatenate([high, low], axis=0)
        S = high.shape[0]
        for b in range(binv.shape[0]):
            cols = slice(b * 128, (b + 1) * 128)
            v = lax.dot_general(both[:, cols], b_high[b], NT, preferred_element_type=F32)
            w = lax.dot_general(high[:, cols], b_low[b], NT, preferred_element_type=F32)
            newest[step, :, pl.ds(b * 128, 128)] = (v[:S] + (v[S:] + w)).astype(newest.dtype)
        out_ref[step] = newest[step]

    near, far = (0, 1, 2, 4), (3, 5, 6, 7)
    partner = pltpu.make_async_remote_copy(newest.at[0], passed, pn_s.at[0], pn_r.at[0],
                                           device_id={"row": shards[3]}, device_id_type=MESH)

    def to_first(k, owner=0):
        where = (tg.at[row, lag] if k in near and not owner else tn.at[shards[owner] // 2, lag])
        return pltpu.make_async_remote_copy(passed if owner else newest.at[0], where,
                                            nb_s.at[k + (owner > 0) * 8], nb_r.at[shards[owner]],
                                            device_id={"lag": 0 if k in near and not owner else 1, "row": shards[k]},
                                            device_id_type=MESH)

    def along_y(n):
        there = (1, 0, 2)[n]
        return pltpu.make_async_remote_copy(newest.at[0], yb.at[there], yb_s.at[n], yb_r.at[there],
                                            device_id={"row": shards[(1, 2, 4)[n]]}, device_id_type=MESH)

    def to_first_y(n, z):
        owner = shards[(1, 2, 4)[n]]
        return pltpu.make_async_remote_copy(yb.at[n], tn.at[owner // 2, lag] if z else tg.at[owner, lag],
                                            nb_s.at[8 + 4 * z + n], nb_r.at[owner],
                                            device_id={"lag": z, "row": shards[3 * z]}, device_id_type=MESH)

    def to_first_own(act):
        @pl.when(zl == 1)
        def _():
            for n in range(3):
                act(along_y(n))
            act(to_first(0))
            act(to_first(3))

        @pl.when(zl == 0)
        def _():
            for k in near[1:]:
                act(to_first(k))

        @pl.when((zl == 0) & (lag > 0))
        def _():
            act(to_first(0))

    def to_first_passed(act):
        @pl.when(zl == 0)
        def _():
            for k in near[1:]:
                act(to_first(k, 3))

        @pl.when((zl == 0) & (lag != 1))
        def _():
            act(to_first(0, 3))

        @pl.when(zl == 1)
        def _():
            for n in range(3):
                for z in range(2):
                    act(to_first_y(n, z))

    def first_wait(k):
        ref = tg.at[shards[k]] if k in near else tn.at[shards[k] // 2]
        if k in (0, 3):
            ref = ref.at[pl.ds(1, 15)]
        pltpu.make_async_remote_copy(ref, ref, nb_s.at[0], nb_r.at[shards[k]], device_id={"lag": 2},
                                     device_id_type=MESH).wait_recv()

    def lend(n):
        k = far[n]
        return pltpu.make_async_remote_copy(mv.at[shards[k]], mv1.at[shards[k] // 2], ln_s.at[n], ln_r.at[n],
                                            device_id={"lag": 1}, device_id_type=MESH)

    def a_shard(k):
        m_loads[k].wait()
        mm(acc, g.at[shards[k]], shards[k], k == 0)

    def t_shard(k):
        mm(acc2, tg.at[shards[k]], shards[k], k == 0)

    a = Gather(lambda s: g.at[s], 16, ga_s, ga_r, 6)
    t = Gather(lambda s: tg.at[s], 16, gt_s, gt_r, 7)

    a.own()

    @pl.when((core == 1) & (lag < 15) & (lag != 7))
    def _():
        shift.start()
    a_shard(0)
    loads[1].wait()
    loads[2].wait()
    b_high[...] = binv[...].astype(b_high.dtype)
    b_low[...] = (binv[...] - b_high[...].astype(F32)).astype(b_low.dtype)
    a.relay1()
    a_shard(1)
    a.relay2()
    @pl.when(lag == 7)
    def _():
        shift.start()
    a_shard(2)
    a.wait(4)
    a_shard(3)
    a.wait(11, 12)
    a_shard(4)
    @pl.when(older & (lag != 8))
    def _():
        shift.wait_recv()
        t.own()
    a.rest(a_shard)
    reduce_send(0)

    @pl.when(core == 0)
    def _():
        for k in range(8):
            sibling_copy(k).start()

    @pl.when(lag == 0)
    def _():
        for n in range(4):
            lend(n).start()

    @pl.when(lag == 8)
    def _():
        shift.wait_recv()
        t.own()
    finish(0)

    @pl.when(zl == 0)
    def _():
        partner.start()
    to_first_own(lambda cp: cp.start())

    @pl.when(zl == 0)
    def _():
        partner.wait_recv()

    @pl.when(zl == 1)
    def _():
        for n in range(3):
            ref = yb.at[n]
            pltpu.make_async_remote_copy(ref, ref, yb_s.at[n], yb_r.at[n], device_id={"lag": 2}, device_id_type=MESH).wait_recv()
    to_first_passed(lambda cp: cp.start())

    @pl.when(core == 1)
    def _():
        for k in range(8):
            sibling_copy(k).wait_recv()
            t_shard(k)

    @pl.when(older)
    def _():
        t_shard(0)
        t.relay1()
        t_shard(1)
        t.relay2()
        t_shard(2)
        t.wait(4)
        t_shard(3)
        t.wait(11, 12)
        t_shard(4)
        t.rest(t_shard)

    @pl.when(lag == 0)
    def _():
        tg[row, 0] = newest[0]
        for n, k in enumerate(near):
            first_wait(k)
            mm(acc2, tg.at[shards[k]], shards[k], n == 0)

    @pl.when(lag == 1)
    def _():
        tn[y, 1] = passed[...]
        for n, k in enumerate(far):
            lend(n).wait_recv()
            first_wait(k)
            mm(acc2, tn.at[shards[k] // 2], shards[k] // 2, False, mv1)

    reduce_send(1)
    finish(1)

    a.drain()
    for step in range(2):
        for k in range(8):
            exchange(step, k).wait_send()
        for k in range(7):
            to_owner(step, k).wait_send()
    to_first_own(lambda cp: cp.wait_send())
    to_first_passed(lambda cp: cp.wait_send())

    @pl.when(zl == 0)
    def _():
        partner.wait_send()

    @pl.when(lag == 0)
    def _():
        for n in range(4):
            lend(n).wait_send()

    @pl.when(older)
    def _():
        t.drain()

    @pl.when(core == 0)
    def _():
        for k in range(8):
            sibling_copy(k).wait_send()

    @pl.when((core == 1) & (lag < 15))
    def _():
        shift.wait_send()


def per_device(lag_matrix, past_current, excitation, block_inverse):
    E, W = past_current.shape[1:]
    S = E // 16
    nb = block_inverse.shape[0]
    bf = past_current.dtype
    dma = pltpu.SemaphoreType.DMA
    past = past_current.reshape(16, S, W)
    return pl.pallas_call(
        kernel,
        out_shape=jax.ShapeDtypeStruct((2, S, W), bf),
        in_specs=[pl.BlockSpec(memory_space=pl.ANY)] * 4,
        out_specs=pl.BlockSpec(memory_space=pltpu.VMEM),
        scratch_shapes=[
            pltpu.VMEM((8, W, W), bf), pltpu.VMEM((8, 16, S, W), bf), pltpu.VMEM((8, 16, S, W), bf),
            pltpu.VMEM((16, S, W), F32), pltpu.VMEM((16, S, W), F32),
            pltpu.VMEM((2, 8, S, W), F32), pltpu.VMEM((2, 8, S, W), F32), pltpu.VMEM((2, 7, S, W), F32),
            pltpu.VMEM((2, S, W), F32), pltpu.VMEM((nb, 128, 128), F32), pltpu.VMEM((2, S, W), bf),
            dma((8,)), dma((3,)), dma((18,)), dma((18,)), dma((18,)), dma((18,)), dma((8,)), dma((8,)),
            dma((1,)), dma((1,)), dma((2, 8)), dma((2, 8)), dma((2, 7)), dma((2, 7)), dma((16,)), dma((8,)),
            pltpu.VMEM((S, W), bf), dma((1,)), dma((1,)), pltpu.VMEM((4, 16, S, W), bf), pltpu.VMEM((4, W, W), bf), dma((4,)), dma((4,)),
            pltpu.VMEM((3, S, W), bf), dma((3,)), dma((3,)), pltpu.VMEM((nb, 128, 128), bf), pltpu.VMEM((nb, 128, 128), bf),
        ],
        compiler_params=pltpu.CompilerParams(collective_id=0, has_side_effects=True, vmem_limit_bytes=60 << 20),
    )(lag_matrix, past, excitation, block_inverse)


def solution(mesh):
    in_specs = (P("lag", "row", None), P("lag", None, "row"), P(None, None, "row"), P("row", None, None))
    return jax.shard_map(per_device, mesh=mesh, in_specs=in_specs, out_specs=P(None, "lag", "row"), check_vma=False)
```
